32 devices in a mesh: frame: 8 (over y, x, core), head: 4 (over z).
Axes of the slice: x: 2, y: 2, z: 4, core: 2. Of those that a mesh axis runs over, the one named last changes fastest.
Arguments:
- visual: bfloat16 [1024, 8192], P('frame'), may hold values from -6 to 6
- w_key: bfloat16 [8192, 1024], P(None, 'head'), may hold values from -0.0625 to 0.0625
- w_value: bfloat16 [8192, 1024], P(None, 'head'), may hold values from -0.0625 to 0.0625
- queries: float32 [256, 8192], P('frame', 'head'), may hold values from -100 to 100
- out_grad: float32 [256, 8192], P('frame', 'head'), may hold values from -6 to 6
Outputs:
- query_grad: float32 [256, 8192], P('frame', 'head')
- key_weight_grad: float32 [8192, 1024], P('frame', 'head')
- value_weight_grad: float32 [8192, 1024], P('frame', 'head')
- visual_grad: float32 [1024, 8192], P('frame', 'head')
The draws below stay inside these ranges and needn't reach their ends.
All inputs are finite; a program needn't handle non-finite values.
Results may differ from the reference program's by a relative error of at most 0.009.
Values sent between devices are 32-bit elements; how exact they have to be, the bound alone decides.
A program may use at most 128 MiB of HBM per device.

```python
import jax
import jax.numpy as jnp
from jax import lax

D = 8192
HEADS = 64
KV_HEADS = 8
HEAD_DIM = 128
VISUAL = 1024
TEXT = 256


def draw_queries(key, part):
    shape = (TEXT, HEADS * HEAD_DIM)
    return jnp.clip(jax.random.normal(jax.random.fold_in(key, 11), shape, jnp.float32), -6.0, 6.0)


def level_of(rng, extent, pieces, low, top_value):
    def one(position, blocks):
        steps = jax.random.uniform(jax.random.fold_in(jax.random.fold_in(rng, 6), position), (blocks,), jnp.float32, low / len(pieces), top_value / len(pieces))
        return jnp.repeat(jnp.exp(steps), extent[position] // blocks).reshape((-1,) + (1,) * (len(extent) - position - 1))

    gain = one(*pieces[0])
    for cut in pieces[1:]:
        gain = gain * one(*cut)
    return gain


def scatter_about(own_key, shape, width, reach, shards=(), kind=jnp.bfloat16):
    drawn = jax.random.normal(own_key, shape, jnp.float32) * width
    if len(shards) > 0:
        drawn = level_of(own_key, shape, shards, -0.22, 0.18) * drawn
    return jnp.clip(drawn, min=-reach, max=reach).astype(kind)


def setup_inputs(seed: int = 0) -> dict:
    splits = jax.random.split(jax.random.key(seed), 6)
    visual = scatter_about(splits[0], (VISUAL, D), 1.0, 6.0, ((0, 8),))
    w_key = scatter_about(splits[1], (D, KV_HEADS * HEAD_DIM), D ** -0.5, 0.0625, ((1, 4),))
    w_value = scatter_about(splits[2], (D, KV_HEADS * HEAD_DIM), D ** -0.5, 0.0625, ((1, 4),))
    queries = draw_queries(jax.random.fold_in(splits[5], 71), 0)
    out_grad = scatter_about(splits[4], (TEXT, HEADS * HEAD_DIM), 1.0, 6.0, ((0, 8), (1, 4)), jnp.float32)
    return {"visual": visual, "w_key": w_key, "w_value": w_value, "queries": queries, "out_grad": out_grad}


def one_group(operands):
    query_blk, grad_blk, key_blk, value_blk = operands
    factor = HEAD_DIM ** -0.5
    scores = jnp.einsum('sgd,nd->gsn', query_blk, key_blk, precision=lax.Precision.HIGHEST) * factor
    top_score = jnp.max(scores, axis=-1, keepdims=True)
    log_total = top_score + jnp.log(jnp.sum(jnp.exp(scores - top_score), axis=-1, keepdims=True))
    probs = jnp.exp(scores - log_total)
    dprob = jnp.einsum('sgd,nd->gsn', grad_blk, value_blk, precision=lax.Precision.HIGHEST)
    delta = jnp.sum(probs * dprob, axis=-1, keepdims=True)
    dscore = probs * (dprob - delta)
    query_part = jnp.einsum('gsn,nd->sgd', dscore, key_blk, precision=lax.Precision.HIGHEST) * factor
    key_part = jnp.einsum('gsn,sgd->nd', dscore, query_blk, precision=lax.Precision.HIGHEST) * factor
    value_part = jnp.einsum('gsn,sgd->nd', probs, grad_blk, precision=lax.Precision.HIGHEST)
    return query_part, key_part, value_part


def reference(visual, w_key, w_value, queries, out_grad):
    keys = jnp.dot(visual, w_key, preferred_element_type=jnp.float32)
    values = jnp.dot(visual, w_value, preferred_element_type=jnp.float32)
    per_group = HEADS // KV_HEADS
    query_heads = queries.reshape(TEXT, KV_HEADS, per_group, HEAD_DIM).transpose(1, 0, 2, 3)
    grad_heads = out_grad.reshape(TEXT, KV_HEADS, per_group, HEAD_DIM).transpose(1, 0, 2, 3)
    key_heads = keys.reshape(VISUAL, KV_HEADS, HEAD_DIM).transpose(1, 0, 2)
    value_heads = values.reshape(VISUAL, KV_HEADS, HEAD_DIM).transpose(1, 0, 2)
    query_part, key_part, value_part = lax.map(one_group, (query_heads, grad_heads, key_heads, value_heads))
    query_grad = query_part.transpose(1, 0, 2, 3).reshape(TEXT, HEADS * HEAD_DIM)
    key_grad = key_part.transpose(1, 0, 2).reshape(VISUAL, KV_HEADS * HEAD_DIM).astype(jnp.bfloat16)
    value_grad = value_part.transpose(1, 0, 2).reshape(VISUAL, KV_HEADS * HEAD_DIM).astype(jnp.bfloat16)
    key_weight_grad = jnp.dot(visual.T, key_grad, preferred_element_type=jnp.float32)
    value_weight_grad = jnp.dot(visual.T, value_grad, preferred_element_type=jnp.float32)
    visual_grad = jnp.dot(key_grad, w_key.T, preferred_element_type=jnp.float32) + jnp.dot(value_grad, w_value.T, preferred_element_type=jnp.float32)
    return query_grad, key_weight_grad, value_weight_grad, visual_grad
```

```python
import functools

import jax
import jax.numpy as jnp
from jax import lax
from jax.experimental import pallas as pl
from jax.experimental.pallas import tpu as pltpu
from jax.sharding import PartitionSpec as P

HEAD_DIM = 128
MESH = pl.DeviceIdType.MESH
CHUNKS = 8
F32, BF16 = jnp.float32, jnp.bfloat16


def halves(a):
    high = a.astype(BF16)
    return high, (a - high.astype(F32)).astype(BF16)


def product(a, b, dims):
    (ah, al), (bh, bl) = a, b
    dot = functools.partial(
        lax.dot_general, dimension_numbers=(dims, ((), ())), preferred_element_type=F32
    )
    return dot(ah, bh) + (dot(ah, bl) + dot(al, bh))


def kernel(
    n, nh, vis, wk_any, wv_any, q, g, qg_out, kwg_out, vwg_out, vg_out,
    wk, wv, visf, visl, vist, ql, gl, kvs, kvl, parts, partl, kgs, agl, qgs, qgl, vgp, vgl,
    w_sem, q_sems, g_sems, kv_sems, v0_sems, v1_sems, part_sems, qg_sems, ag_sems, z_sems,
):
    me, my_head = lax.axis_index("frame"), lax.axis_index("head")
    rows, depth = vis.shape
    cols = wk.shape[1]
    kv_local = cols // HEAD_DIM
    text_part, width = ql.shape[1], ql.shape[2]
    split = q.shape[0] // text_part
    heads = width // HEAD_DIM
    share = n // kv_local
    dn, dh = depth // n, depth // nh
    chunk = depth // CHUNKS
    half = rows // 2
    factor = HEAD_DIM ** (-0.5)

    def frame_copy(src, dst, sems, slot_send, slot_recv, target):
        return pltpu.make_async_remote_copy(
            src_ref=src, dst_ref=dst, send_sem=sems.at[0, slot_send],
            recv_sem=sems.at[1, slot_recv], device_id={"frame": target}, device_id_type=MESH,
        )

    def peer(k):
        return lax.rem(me + k, n)

    def source(k):
        return lax.rem(me + n - k, n)

    loads = []
    for c in range(CHUNKS):
        at = pl.ds(c * chunk, chunk)
        for i, (src, dst) in enumerate(((wk_any, wk), (wv_any, wv))):
            loads.append(pltpu.make_async_copy(src.at[at], dst.at[at], w_sem.at[i, c]))
            loads[-1].start()

    barrier = pltpu.get_barrier_semaphore()
    for k in range(1, n):
        pl.semaphore_signal(barrier, inc=1, device_id={"frame": peer(k)}, device_id_type=MESH)
    for j in range(1, nh):
        pl.semaphore_signal(
            barrier, inc=1, device_id={"head": lax.rem(my_head + j, nh)}, device_id_type=MESH
        )
    pl.semaphore_wait(barrier, n + nh - 2)

    def text_at(p):
        part, block = lax.rem(p, split), p // split
        return (
            pl.ds(pl.multiple_of(part * text_part, text_part), text_part),
            pl.ds(pl.multiple_of(block * width, width), width),
        )

    sends = []
    for k in range(1, n):
        p = peer(k)
        for src, dst, sems in ((q, ql, q_sems), (g, gl, g_sems)):
            sends.append(frame_copy(src.at[text_at(p)], dst.at[me], sems, p, me, p))
            sends[-1].start()
    ql[me] = q[text_at(me)]
    gl[me] = g[text_at(me)]

    acc_k = acc_v = jnp.zeros((rows, cols), F32)
    for c in range(CHUNKS):
        loads[2 * c].wait()
        loads[2 * c + 1].wait()
        at = pl.ds(c * chunk, chunk)
        acc_k += jnp.dot(vis[:, at], wk[at], preferred_element_type=F32)
        acc_v += jnp.dot(vis[:, at], wv[at], preferred_element_type=F32)
    for a in range(kv_local):
        at = slice(a * HEAD_DIM, (a + 1) * HEAD_DIM)
        kvs[a, 0] = acc_k[:, at]
        kvs[a, 1] = acc_v[:, at]
    for k in range(1, n):
        p = peer(k)
        sends.append(frame_copy(kvs.at[p // share], kvl.at[me], kv_sems, p, me, p))
        sends[-1].start()
    kvl[me] = kvs[me // share]

    for p in range(n):
        visf[p] = vis[:, p * dn : (p + 1) * dn].astype(F32)

    def send_visual(first, sems):
        at = pl.ds(first, half)
        for k in range(1, n):
            p = peer(k)
            sends.append(frame_copy(visf.at[p, at], visl.at[me, at], sems, p, me, p))
            sends[-1].start()

    send_visual(0, v0_sems)

    def wait_all(land, sems):
        for k in range(1, n):
            s = source(k)
            frame_copy(land.at[s], land.at[s], sems, s, s, s).wait_recv()

    wait_all(ql, q_sems)
    wait_all(gl, g_sems)
    wait_all(kvl, kv_sems)

    keys = kvl[:, 0].reshape(n * rows, HEAD_DIM)
    values = kvl[:, 1].reshape(n * rows, HEAD_DIM)
    values2 = halves(values)
    keys_t = halves(keys.T)
    key_part = value_part = None
    for h in range(heads):
        at = slice(h * HEAD_DIM, (h + 1) * HEAD_DIM)
        query = ql[:, :, at].reshape(n * text_part, HEAD_DIM)
        grad = gl[:, :, at].reshape(n * text_part, HEAD_DIM)
        query2, grad2 = halves(query), halves(grad)
        scores = lax.dot_general(
            keys, query, (((1,), (1,)), ((), ())),
            precision=lax.Precision.HIGHEST, preferred_element_type=F32,
        ) * factor
        probs = jnp.exp(scores - jnp.max(scores, axis=0, keepdims=True))
        probs = probs * (1.0 / jnp.sum(probs, axis=0, keepdims=True))
        dprob = product(values2, grad2, ((1,), (1,)))
        delta = jnp.sum(probs * dprob, axis=0, keepdims=True)
        dscore2 = halves(probs * (dprob - delta))
        key_term = product(dscore2, query2, ((1,), (0,)))
        value_term = product(halves(probs), grad2, ((1,), (0,)))
        key_part = key_term if h == 0 else key_part + key_term
        value_part = value_term if h == 0 else value_part + value_term
        query_term = product(keys_t, dscore2, ((1,), (0,))).T * factor
        qgs[:, :, at] = query_term.reshape(n, text_part, HEAD_DIM)
    parts[:, 0] = key_part.reshape(n, rows, HEAD_DIM)
    parts[:, 1] = value_part.reshape(n, rows, HEAD_DIM)
    for k in range(1, n):
        p = peer(k)
        sends.append(frame_copy(parts.at[p], partl.at[me], part_sems, p, me, p))
        sends[-1].start()
    partl[me] = parts[me]
    send_visual(half, v1_sems)

    wait_all(partl, part_sems)
    low = []
    for i in range(2):
        columns = []
        for a in range(kv_local):
            total = partl[a * share, i]
            for p in range(a * share + 1, (a + 1) * share):
                total = total + partl[p, i]
            columns.append(total * factor if i == 0 else total)
        for a in range(kv_local):
            kgs[i, :, a * HEAD_DIM : (a + 1) * HEAD_DIM] = columns[a].astype(BF16).astype(F32)
        low.append(kgs[i].astype(BF16))

    def visual_term(p):
        at = pl.ds(pl.multiple_of(p * dh, dh), dh)
        dims = (((1,), (1,)), ((), ()))
        return lax.dot_general(
            low[0], wk[at], dims, preferred_element_type=F32
        ) + lax.dot_general(low[1], wv[at], dims, preferred_element_type=F32)

    order = sorted(range(1, nh), key=lambda j: -min(j, nh - j))
    for j in order:
        p = lax.rem(my_head + j, nh)
        vgp[p] = visual_term(p)
        sends.append(
            pltpu.make_async_remote_copy(
                src_ref=vgp.at[p], dst_ref=vgl.at[my_head], send_sem=z_sems.at[0, p],
                recv_sem=z_sems.at[1, my_head], device_id={"head": p}, device_id_type=MESH,
            )
        )
        sends[-1].start()
    for k in range(1, n):
        p = peer(k)
        sends.append(frame_copy(kgs, agl.at[me], ag_sems, p, me, p))
        sends[-1].start()
    for k in range(1, n):
        p = peer(k)
        sends.append(frame_copy(qgs.at[p], qgl.at[me], qg_sems, p, me, p))
        sends[-1].start()
    qgl[me] = qgs[me]
    agl[me] = kgs[...]
    vgl[my_head] = visual_term(my_head)

    def columns_of(s):
        return pl.ds(pl.multiple_of(s * rows, rows), rows)

    vist[:, columns_of(me)] = visf[me].T.astype(BF16)
    for k in range(1, n):
        s = source(k)
        for first, sems in ((0, v0_sems), (half, v1_sems)):
            land = visl.at[s, pl.ds(first, half)]
            frame_copy(land, land, sems, s, s, s).wait_recv()
        vist[:, columns_of(s)] = visl[s].T.astype(BF16)

    wait_all(agl, ag_sems)
    for i, out in enumerate((kwg_out, vwg_out)):
        out[...] = jnp.dot(
            vist[...], agl[:, i].reshape(n * rows, cols).astype(BF16), preferred_element_type=F32
        )
    wait_all(qgl, qg_sems)
    for s in range(n):
        part, block = s % split, s // split
        qg_out[
            part * text_part : (part + 1) * text_part, block * width : (block + 1) * width
        ] = qgl[s]

    for j in range(1, nh):
        s = lax.rem(my_head + nh - j, nh)
        pltpu.make_async_remote_copy(
            src_ref=vgl.at[s], dst_ref=vgl.at[s], send_sem=z_sems.at[0, s],
            recv_sem=z_sems.at[1, s], device_id={"head": s}, device_id_type=MESH,
        ).wait_recv()
    total = vgl[0]
    for p in range(1, nh):
        total = total + vgl[p]
    vg_out[...] = total
    for copy in sends:
        copy.wait_send()


def solution(mesh):
    n, nh = mesh.shape["frame"], mesh.shape["head"]

    def body(visual, w_key, w_value, queries, out_grad):
        rows, depth = visual.shape
        cols = w_key.shape[1]
        text, query_cols = queries.shape
        local_heads = query_cols // HEAD_DIM
        split = max(1, n // local_heads)
        part, width = text // split, query_cols * split // n
        vmem = pl.BlockSpec(memory_space=pltpu.VMEM)
        hbm = pl.BlockSpec(memory_space=pl.ANY)
        dn, dh = depth // n, depth // nh
        pairs = pltpu.SemaphoreType.DMA((2, n))
        return pl.pallas_call(
            functools.partial(kernel, n, nh),
            out_shape=(
                jax.ShapeDtypeStruct((text, query_cols), F32),
                jax.ShapeDtypeStruct((dn, cols), F32),
                jax.ShapeDtypeStruct((dn, cols), F32),
                jax.ShapeDtypeStruct((rows, dh), F32),
            ),
            in_specs=[vmem, hbm, hbm, vmem, vmem],
            out_specs=(vmem, vmem, vmem, vmem),
            scratch_shapes=[
                pltpu.VMEM((depth, cols), BF16),
                pltpu.VMEM((depth, cols), BF16),
                pltpu.VMEM((n, rows, dn), F32),
                pltpu.VMEM((n, rows, dn), F32),
                pltpu.VMEM((dn, n * rows), BF16),
                pltpu.VMEM((n, part, width), F32),
                pltpu.VMEM((n, part, width), F32),
                pltpu.VMEM((cols // HEAD_DIM, 2, rows, HEAD_DIM), F32),
                pltpu.VMEM((n, 2, rows, HEAD_DIM), F32),
                pltpu.VMEM((n, 2, rows, HEAD_DIM), F32),
                pltpu.VMEM((n, 2, rows, HEAD_DIM), F32),
                pltpu.VMEM((2, rows, cols), F32),
                pltpu.VMEM((n, 2, rows, cols), F32),
                pltpu.VMEM((n, part, width), F32),
                pltpu.VMEM((n, part, width), F32),
                pltpu.VMEM((nh, rows, dh), F32),
                pltpu.VMEM((nh, rows, dh), F32),
                pltpu.SemaphoreType.DMA((2, CHUNKS)),
                pairs, pairs, pairs, pairs, pairs, pairs, pairs, pairs,
                pltpu.SemaphoreType.DMA((2, nh)),
            ],
            compiler_params=pltpu.CompilerParams(
                collective_id=0, has_side_effects=True, vmem_limit_bytes=67000000
            ),
        )(visual, w_key, w_value, queries, out_grad)

    return jax.shard_map(
        body,
        mesh=mesh,
        in_specs=(
            P("frame", None),
            P(None, "head"),
            P(None, "head"),
            P("frame", "head"),
            P("frame", "head"),
        ),
        out_specs=(P("frame", "head"), P("frame", "head"), P("frame", "head"), P("frame", "head")),
        check_vma=False,
    )
```

```python
import functools

import jax
import jax.numpy as jnp
from jax import lax
from jax.experimental import pallas as pl
from jax.experimental.pallas import tpu as pltpu
from jax.sharding import PartitionSpec as P

HEAD_DIM = 128
MESH = pl.DeviceIdType.MESH
CHUNKS = 8
PIECES = 4
F32, BF16 = jnp.float32, jnp.bfloat16


def halves(a):
    high = a.astype(BF16)
    return high, (a - high.astype(F32)).astype(BF16)


def product(a, b, dims):
    (ah, al), (bh, bl) = a, b
    dot = functools.partial(
        lax.dot_general, dimension_numbers=(dims, ((), ())), preferred_element_type=F32
    )
    return dot(ah, bh) + (dot(ah, bl) + dot(al, bh))


def kernel(
    n, nh, vis, wk_any, wv_any, q, g, qg_out, kwg_out, vwg_out, vg_out,
    wk, wv, visf, visl, vist, ql, gl, kvs, kvl, parts, partl, kgs, agl, qgs, qgl, vgp, zr, zl,
    w_sem, q_sems, g_sems, kv_sems, v_sems, part_sems, qg_sems, ag_sems, z_sems,
):
    me, my_head = lax.axis_index("frame"), lax.axis_index("head")
    rows, depth = vis.shape
    cols = wk.shape[1]
    kv_local = cols // HEAD_DIM
    text_part, width = ql.shape[1], ql.shape[2]
    split = q.shape[0] // text_part
    heads = width // HEAD_DIM
    share = n // kv_local
    dn, dh = depth // n, depth // nh
    chunk = depth // CHUNKS
    bounds = (0, rows // 8, rows // 4, rows)
    piece = rows // PIECES
    factor = HEAD_DIM ** (-0.5)

    def frame_copy(src, dst, sems, slot_send, slot_recv, target):
        return pltpu.make_async_remote_copy(
            src_ref=src, dst_ref=dst, send_sem=sems.at[0, slot_send],
            recv_sem=sems.at[1, slot_recv], device_id={"frame": target}, device_id_type=MESH,
        )

    def peer(k):
        return lax.rem(me + k, n)

    def source(k):
        return lax.rem(me + n - k, n)

    loads = []
    for c in range(CHUNKS):
        at = pl.ds(c * chunk, chunk)
        for i, (src, dst) in enumerate(((wk_any, wk), (wv_any, wv))):
            loads.append(pltpu.make_async_copy(src.at[at], dst.at[at], w_sem.at[i, c]))
            loads[-1].start()

    barrier = pltpu.get_barrier_semaphore()
    for k in range(1, n):
        pl.semaphore_signal(barrier, inc=1, device_id={"frame": peer(k)}, device_id_type=MESH)
    for j in range(1, nh):
        pl.semaphore_signal(
            barrier, inc=1, device_id={"head": lax.rem(my_head + j, nh)}, device_id_type=MESH
        )
    pl.semaphore_wait(barrier, n + nh - 2)

    def text_at(p):
        part, block = lax.rem(p, split), p // split
        return (
            pl.ds(pl.multiple_of(part * text_part, text_part), text_part),
            pl.ds(pl.multiple_of(block * width, width), width),
        )

    sends = []
    for k in range(1, n):
        p = peer(k)
        for src, dst, sems in ((q, ql, q_sems), (g, gl, g_sems)):
            sends.append(frame_copy(src.at[text_at(p)], dst.at[me], sems, p, me, p))
            sends[-1].start()
    ql[me] = q[text_at(me)]
    gl[me] = g[text_at(me)]

    for p in range(n):
        visf[p] = vis[:, p * dn : (p + 1) * dn].astype(F32)

    def stretch(i):
        return pl.ds(bounds[i], bounds[i + 1] - bounds[i])

    def send_visual(i):
        for k in range(1, n):
            p = peer(k)
            sends.append(
                frame_copy(
                    visf.at[p, stretch(i)], visl.at[me, stretch(i)], v_sems.at[i], p, me, p
                )
            )
            sends[-1].start()

    send_visual(0)

    acc_k = acc_v = jnp.zeros((rows, cols), F32)
    for c in range(CHUNKS):
        loads[2 * c].wait()
        loads[2 * c + 1].wait()
        at = pl.ds(c * chunk, chunk)
        acc_k += jnp.dot(vis[:, at], wk[at], preferred_element_type=F32)
        acc_v += jnp.dot(vis[:, at], wv[at], preferred_element_type=F32)
    for a in range(kv_local):
        at = slice(a * HEAD_DIM, (a + 1) * HEAD_DIM)
        kvs[a, 0] = acc_k[:, at]
        kvs[a, 1] = acc_v[:, at]
    for k in range(1, n):
        p = peer(k)
        sends.append(frame_copy(kvs.at[p // share], kvl.at[me], kv_sems, p, me, p))
        sends[-1].start()
    kvl[me] = kvs[me // share]

    send_visual(1)

    def wait_all(land, sems):
        for k in range(1, n):
            s = source(k)
            frame_copy(land.at[s], land.at[s], sems, s, s, s).wait_recv()

    wait_all(ql, q_sems)
    wait_all(gl, g_sems)
    wait_all(kvl, kv_sems)

    keys = kvl[:, 0].reshape(n * rows, HEAD_DIM)
    values = kvl[:, 1].reshape(n * rows, HEAD_DIM)
    values2 = halves(values)
    keys_t = halves(keys.T)
    key_part = value_part = None
    for h in range(heads):
        at = slice(h * HEAD_DIM, (h + 1) * HEAD_DIM)
        query = ql[:, :, at].reshape(n * text_part, HEAD_DIM)
        grad = gl[:, :, at].reshape(n * text_part, HEAD_DIM)
        query2, grad2 = halves(query), halves(grad)
        scores = lax.dot_general(
            keys, query, (((1,), (1,)), ((), ())),
            precision=lax.Precision.HIGHEST, preferred_element_type=F32,
        ) * factor
        probs = jnp.exp(scores - jnp.max(scores, axis=0, keepdims=True))
        probs = probs * (1.0 / jnp.sum(probs, axis=0, keepdims=True))
        dprob = product(values2, grad2, ((1,), (1,)))
        delta = jnp.sum(probs * dprob, axis=0, keepdims=True)
        dscore2 = halves(probs * (dprob - delta))
        key_term = product(dscore2, query2, ((1,), (0,)))
        value_term = product(halves(probs), grad2, ((1,), (0,)))
        key_part = key_term if h == 0 else key_part + key_term
        value_part = value_term if h == 0 else value_part + value_term
        query_term = product(keys_t, dscore2, ((1,), (0,))).T * factor
        qgs[:, :, at] = query_term.reshape(n, text_part, HEAD_DIM)
    parts[:, 0] = key_part.reshape(n, rows, HEAD_DIM)
    parts[:, 1] = value_part.reshape(n, rows, HEAD_DIM)
    for k in range(1, n):
        p = peer(k)
        sends.append(frame_copy(parts.at[p], partl.at[me], part_sems, p, me, p))
        sends[-1].start()
    partl[me] = parts[me]
    for k in range(1, n):
        p = peer(k)
        sends.append(frame_copy(qgs.at[p], qgl.at[me], qg_sems, p, me, p))
        sends[-1].start()
    qgl[me] = qgs[me]
    send_visual(2)

    wait_all(partl, part_sems)
    low = []
    for i in range(2):
        columns = []
        for a in range(kv_local):
            total = partl[a * share, i]
            for p in range(a * share + 1, (a + 1) * share):
                total = total + partl[p, i]
            columns.append(total * factor if i == 0 else total)
        for a in range(kv_local):
            kgs[i, :, a * HEAD_DIM : (a + 1) * HEAD_DIM] = columns[a].astype(BF16).astype(F32)
        low.append(kgs[i].astype(BF16))

    for k in range(1, n):
        p = peer(k)
        sends.append(frame_copy(kgs, agl.at[me], ag_sems, p, me, p))
        sends[-1].start()
    agl[me] = kgs[...]

    def visual_term(p):
        at = slice(p * dh, (p + 1) * dh)
        dims = (((1,), (1,)), ((), ()))
        vgp[p] = lax.dot_general(
            low[0], wk[at], dims, preferred_element_type=F32
        ) + lax.dot_general(low[1], wv[at], dims, preferred_element_type=F32)

    def hop(way, d, i):
        at = pl.ds(i * piece, piece)
        land = zr if way == 0 else zl
        return pltpu.make_async_remote_copy(
            src_ref=vgp.at[d, at], dst_ref=land.at[d, at], send_sem=z_sems.at[way, 0, d, i],
            recv_sem=z_sems.at[way, 1, d, i], device_id_type=MESH,
            device_id={"head": jnp.clip(my_head + 1 - 2 * way, 0, nh - 1)},
        )

    def sends_to(way, d):
        return my_head < d if way == 0 else my_head > d

    def takes_from(way):
        return my_head > 0 if way == 0 else my_head < nh - 1

    def relay(way, d, i):
        at = pl.ds(i * piece, piece)
        land = zr if way == 0 else zl

        @pl.when(sends_to(way, d))
        def _():
            @pl.when(takes_from(way))
            def _():
                hop(way, d, i).wait_recv()
                vgp[d, at] += land[d, at]

            hop(way, d, i).start()

    def columns_of(s):
        return pl.ds(pl.multiple_of(s * rows, rows), rows)

    def take_visual(k):
        s = source(k)
        for i in range(3):
            land = visl.at[s, stretch(i)]
            frame_copy(land, land, v_sems.at[i], s, s, s).wait_recv()
        vist[:, columns_of(s)] = visl[s].T.astype(BF16)

    vist[:, columns_of(me)] = visf[me].T.astype(BF16)
    far = range(nh - 1, 0, -1)
    left = list(range(1, n))
    done = set()
    for step, d in enumerate(far):
        for way, at in ((0, d), (1, nh - 1 - d)):
            if at not in done:
                visual_term(at)
                done.add(at)
        for i in range(PIECES):
            for way, at in ((0, d), (1, nh - 1 - d)):
                relay(way, at, i)
    for k in left:
        take_visual(k)

    wait_all(agl, ag_sems)
    for i, out in enumerate((kwg_out, vwg_out)):
        out[...] = jnp.dot(
            vist[...], agl[:, i].reshape(n * rows, cols).astype(BF16), preferred_element_type=F32
        )
    wait_all(qgl, qg_sems)
    for s in range(n):
        part, block = s % split, s // split
        qg_out[
            part * text_part : (part + 1) * text_part, block * width : (block + 1) * width
        ] = qgl[s]

    vg_out[...] = vgp[my_head]
    for way, land in ((0, zr), (1, zl)):

        @pl.when(takes_from(way))
        def _():
            for i in range(PIECES):
                hop(way, my_head, i).wait_recv()
            vg_out[...] += land[my_head]

        for d in range(nh):

            @pl.when(sends_to(way, d))
            def _():
                for i in range(PIECES):
                    hop(way, d, i).wait_send()

    for copy in sends:
        copy.wait_send()


def solution(mesh):
    n, nh = mesh.shape["frame"], mesh.shape["head"]

    def body(visual, w_key, w_value, queries, out_grad):
        rows, depth = visual.shape
        cols = w_key.shape[1]
        text, query_cols = queries.shape
        local_heads = query_cols // HEAD_DIM
        split = max(1, n // local_heads)
        part, width = text // split, query_cols * split // n
        vmem = pl.BlockSpec(memory_space=pltpu.VMEM)
        hbm = pl.BlockSpec(memory_space=pl.ANY)
        dn, dh = depth // n, depth // nh
        pairs = pltpu.SemaphoreType.DMA((2, n))
        return pl.pallas_call(
            functools.partial(kernel, n, nh),
            out_shape=(
                jax.ShapeDtypeStruct((text, query_cols), F32),
                jax.ShapeDtypeStruct((dn, cols), F32),
                jax.ShapeDtypeStruct((dn, cols), F32),
                jax.ShapeDtypeStruct((rows, dh), F32),
            ),
            in_specs=[vmem, hbm, hbm, vmem, vmem],
            out_specs=(vmem, vmem, vmem, vmem),
            scratch_shapes=[
                pltpu.VMEM((depth, cols), BF16),
                pltpu.VMEM((depth, cols), BF16),
                pltpu.VMEM((n, rows, dn), F32),
                pltpu.VMEM((n, rows, dn), F32),
                pltpu.VMEM((dn, n * rows), BF16),
                pltpu.VMEM((n, part, width), F32),
                pltpu.VMEM((n, part, width), F32),
                pltpu.VMEM((cols // HEAD_DIM, 2, rows, HEAD_DIM), F32),
                pltpu.VMEM((n, 2, rows, HEAD_DIM), F32),
                pltpu.VMEM((n, 2, rows, HEAD_DIM), F32),
                pltpu.VMEM((n, 2, rows, HEAD_DIM), F32),
                pltpu.VMEM((2, rows, cols), F32),
                pltpu.VMEM((n, 2, rows, cols), F32),
                pltpu.VMEM((n, part, width), F32),
                pltpu.VMEM((n, part, width), F32),
                pltpu.VMEM((nh, rows, dh), F32),
                pltpu.VMEM((nh, rows, dh), F32),
                pltpu.VMEM((nh, rows, dh), F32),
                pltpu.SemaphoreType.DMA((2, CHUNKS)),
                pairs, pairs, pairs,
                pltpu.SemaphoreType.DMA((3, 2, n)),
                pairs, pairs, pairs,
                pltpu.SemaphoreType.DMA((2, 2, nh, PIECES)),
            ],
            compiler_params=pltpu.CompilerParams(
                collective_id=0, has_side_effects=True, vmem_limit_bytes=67000000
            ),
        )(visual, w_key, w_value, queries, out_grad)

    return jax.shard_map(
        body,
        mesh=mesh,
        in_specs=(
            P("frame", None),
            P(None, "head"),
            P(None, "head"),
            P("frame", "head"),
            P("frame", "head"),
        ),
        out_specs=(P("frame", "head"), P("frame", "head"), P("frame", "head"), P("frame", "head")),
        check_vma=False,
    )
```

```python
import functools

import jax
import jax.numpy as jnp
from jax import lax
from jax.experimental import pallas as pl
from jax.experimental.pallas import tpu as pltpu
from jax.sharding import PartitionSpec as P

HEAD_DIM = 128
MESH = pl.DeviceIdType.MESH
CHUNKS = 8
PIECES = 4
F32, BF16 = jnp.float32, jnp.bfloat16


def halves(a):
    high = a.astype(BF16)
    return high, (a - high.astype(F32)).astype(BF16)


def product(a, b, dims):
    (ah, al), (bh, bl) = a, b
    dot = functools.partial(
        lax.dot_general, dimension_numbers=(dims, ((), ())), preferred_element_type=F32
    )
    return dot(ah, bh) + (dot(ah, bl) + dot(al, bh))


def kernel(
    n, nh, vis, wk_any, wv_any, q, g, qg_out, kwg_out, vwg_out, vg_out,
    wk, wv, visf, visl, vist, ql, gl, kvs, kvl, parts, pre, partl, kgs, agl, qgs, qgl, vgp, zr, zl,
    w_sem, q_sems, g_sems, kv_sems, v_sems, pre_sem, part_sems, qg_sems, ag_sems, on_sems, z_sems,
):
    me, my_head = lax.axis_index("frame"), lax.axis_index("head")
    rows, depth = vis.shape
    cols = wk.shape[1]
    kv_local = cols // HEAD_DIM
    text_part, width = ql.shape[1], ql.shape[2]
    split = q.shape[0] // text_part
    heads = width // HEAD_DIM
    share = n // kv_local
    dn, dh = depth // n, depth // nh
    chunk = depth // CHUNKS
    bounds = (0, rows // 8, rows // 4, rows)
    piece = rows // PIECES
    factor = HEAD_DIM ** (-0.5)

    def frame_copy(src, dst, sems, slot_send, slot_recv, target):
        return pltpu.make_async_remote_copy(
            src_ref=src, dst_ref=dst, send_sem=sems.at[0, slot_send],
            recv_sem=sems.at[1, slot_recv], device_id={"frame": target}, device_id_type=MESH,
        )

    def frame_copy_of(src, dst, send_sem, recv_sem, target):
        return pltpu.make_async_remote_copy(
            src_ref=src, dst_ref=dst, send_sem=send_sem, recv_sem=recv_sem,
            device_id={"frame": target}, device_id_type=MESH,
        )

    def peer(k):
        return lax.rem(me + k, n)

    def source(k):
        return lax.rem(me + n - k, n)

    core, chip, chips = lax.rem(me, 2), me // 2, n // 2
    sibling = me + 1 - 2 * core

    def mate(j):
        return lax.rem(me + 2 * j, n)

    def mate_source(j):
        return lax.rem(me + n - 2 * j, n)

    def onward(land, sems, on, s):
        return frame_copy_of(land.at[s], land.at[s], on.at[s], sems.at[1, s], sibling)

    def spread(pick, land, sems):
        sends.append(frame_copy(pick(sibling), land.at[me], sems, sibling, me, sibling))
        sends[-1].start()
        for j in range(1, chips):
            p = mate(j)
            sends.append(frame_copy(pick(p), land.at[me], sems, p, me, p))
            sends[-1].start()

    def forward(land, sems, on):
        for j in range(1, chips):
            s = mate_source(j)
            frame_copy(land.at[s], land.at[s], sems, s, s, s).wait_recv()
            sends.append(onward(land, sems, on, s))
            sends[-1].start()

    def wait_rest(land, sems):
        frame_copy(land.at[sibling], land.at[sibling], sems, sibling, sibling, sibling).wait_recv()
        for j in range(1, chips):
            s = lax.rem(sibling + n - 2 * j, n)
            frame_copy(land.at[s], land.at[s], sems, s, s, sibling).wait_recv()

    loads = []
    for c in range(CHUNKS):
        at = pl.ds(c * chunk, chunk)
        for i, (src, dst) in enumerate(((wk_any, wk), (wv_any, wv))):
            loads.append(pltpu.make_async_copy(src.at[at], dst.at[at], w_sem.at[i, c]))
            loads[-1].start()

    barrier = pltpu.get_barrier_semaphore()
    for k in range(1, n):
        pl.semaphore_signal(barrier, inc=1, device_id={"frame": peer(k)}, device_id_type=MESH)
    for j in range(1, nh):
        pl.semaphore_signal(
            barrier, inc=1, device_id={"head": lax.rem(my_head + j, nh)}, device_id_type=MESH
        )
    pl.semaphore_wait(barrier, n + nh - 2)

    def text_at(p):
        part, block = lax.rem(p, split), p // split
        return (
            pl.ds(pl.multiple_of(part * text_part, text_part), text_part),
            pl.ds(pl.multiple_of(block * width, width), width),
        )

    sends = []
    for k in range(1, n):
        p = peer(k)
        for src, dst, sems in ((q, ql, q_sems), (g, gl, g_sems)):
            sends.append(frame_copy(src.at[text_at(p)], dst.at[me], sems, p, me, p))
            sends[-1].start()
    ql[me] = q[text_at(me)]
    gl[me] = g[text_at(me)]

    for p in range(n):
        visf[p] = vis[:, p * dn : (p + 1) * dn].astype(F32)

    def stretch(i):
        return pl.ds(bounds[i], bounds[i + 1] - bounds[i])

    def send_visual(i):
        for k in range(1, n):
            p = peer(k)
            sends.append(
                frame_copy(
                    visf.at[p, stretch(i)], visl.at[me, stretch(i)], v_sems.at[i], p, me, p
                )
            )
            sends[-1].start()

    send_visual(0)

    acc_k = acc_v = jnp.zeros((rows, cols), F32)
    for c in range(CHUNKS):
        loads[2 * c].wait()
        loads[2 * c + 1].wait()
        at = pl.ds(c * chunk, chunk)
        acc_k += jnp.dot(vis[:, at], wk[at], preferred_element_type=F32)
        acc_v += jnp.dot(vis[:, at], wv[at], preferred_element_type=F32)
    for a in range(kv_local):
        at = slice(a * HEAD_DIM, (a + 1) * HEAD_DIM)
        kvs[a, 0] = acc_k[:, at]
        kvs[a, 1] = acc_v[:, at]
    spread(lambda p: kvs.at[p // share], kvl, kv_sems)
    kvl[me] = kvs[me // share]

    send_visual(1)

    def wait_all(land, sems):
        for k in range(1, n):
            s = source(k)
            frame_copy(land.at[s], land.at[s], sems, s, s, s).wait_recv()

    forward(kvl, kv_sems, on_sems.at[0])
    wait_all(ql, q_sems)
    wait_all(gl, g_sems)
    wait_rest(kvl, kv_sems)

    keys = kvl[:, 0].reshape(n * rows, HEAD_DIM)
    values = kvl[:, 1].reshape(n * rows, HEAD_DIM)
    values2 = halves(values)
    keys_t = halves(keys.T)
    key_part = value_part = None
    for h in range(heads):
        at = slice(h * HEAD_DIM, (h + 1) * HEAD_DIM)
        query = ql[:, :, at].reshape(n * text_part, HEAD_DIM)
        grad = gl[:, :, at].reshape(n * text_part, HEAD_DIM)
        query2, grad2 = halves(query), halves(grad)
        scores = lax.dot_general(
            keys, query, (((1,), (1,)), ((), ())),
            precision=lax.Precision.HIGHEST, preferred_element_type=F32,
        ) * factor
        probs = jnp.exp(scores - jnp.max(scores, axis=0, keepdims=True))
        probs = probs * (1.0 / jnp.sum(probs, axis=0, keepdims=True))
        dprob = product(values2, grad2, ((1,), (1,)))
        delta = jnp.sum(probs * dprob, axis=0, keepdims=True)
        dscore2 = halves(probs * (dprob - delta))
        key_term = product(dscore2, query2, ((1,), (0,)))
        value_term = product(halves(probs), grad2, ((1,), (0,)))
        key_part = key_term if h == 0 else key_part + key_term
        value_part = value_term if h == 0 else value_part + value_term
        query_term = product(keys_t, dscore2, ((1,), (0,))).T * factor
        qgs[:, :, at] = query_term.reshape(n, text_part, HEAD_DIM)
    for i, part in enumerate((key_part, value_part)):
        part = part.reshape(chips, 2, rows, HEAD_DIM)
        for c in range(2):
            parts[c, :, i] = part[:, c]
    exchange = frame_copy_of(
        parts.at[1 - core], pre, pre_sem.at[0], pre_sem.at[1], sibling
    )
    exchange.start()
    exchange.wait_recv()
    sends.append(exchange)
    parts[core] += pre[...]
    for j in range(1, chips):
        p = mate(j)
        sends.append(
            frame_copy(parts.at[core, p // 2], partl.at[chip], part_sems, p // 2, chip, p)
        )
        sends[-1].start()
    partl[chip] = parts[core, chip]
    for k in range(1, n):
        p = peer(k)
        sends.append(frame_copy(qgs.at[p], qgl.at[me], qg_sems, p, me, p))
        sends[-1].start()
    qgl[me] = qgs[me]
    send_visual(2)

    for j in range(1, chips):
        s = mate_source(j)
        land = partl.at[s // 2]
        frame_copy(land, land, part_sems, s // 2, s // 2, s).wait_recv()
    low = []
    for i in range(2):
        columns = []
        for a in range(kv_local):
            total = partl[a * share // 2, i]
            for p in range(a * share // 2 + 1, (a + 1) * share // 2):
                total = total + partl[p, i]
            columns.append(total * factor if i == 0 else total)
        for a in range(kv_local):
            kgs[i, :, a * HEAD_DIM : (a + 1) * HEAD_DIM] = columns[a].astype(BF16).astype(F32)
        low.append(kgs[i].astype(BF16))

    spread(lambda p: kgs, agl, ag_sems)
    agl[me] = kgs[...]

    def visual_term(p):
        at = slice(p * dh, (p + 1) * dh)
        dims = (((1,), (1,)), ((), ()))
        vgp[p] = lax.dot_general(
            low[0], wk[at], dims, preferred_element_type=F32
        ) + lax.dot_general(low[1], wv[at], dims, preferred_element_type=F32)

    def hop(way, d, i):
        at = pl.ds(i * piece, piece)
        land = zr if way == 0 else zl
        return pltpu.make_async_remote_copy(
            src_ref=vgp.at[d, at], dst_ref=land.at[d, at], send_sem=z_sems.at[way, 0, d, i],
            recv_sem=z_sems.at[way, 1, d, i], device_id_type=MESH,
            device_id={"head": jnp.clip(my_head + 1 - 2 * way, 0, nh - 1)},
        )

    def sends_to(way, d):
        return my_head < d if way == 0 else my_head > d

    def takes_from(way):
        return my_head > 0 if way == 0 else my_head < nh - 1

    def relay(way, d, i):
        at = pl.ds(i * piece, piece)
        land = zr if way == 0 else zl

        @pl.when(sends_to(way, d))
        def _():
            @pl.when(takes_from(way))
            def _():
                hop(way, d, i).wait_recv()
                vgp[d, at] += land[d, at]

            hop(way, d, i).start()

    def columns_of(s):
        return pl.ds(pl.multiple_of(s * rows, rows), rows)

    def take_visual(k):
        s = source(k)
        for i in range(3):
            land = visl.at[s, stretch(i)]
            frame_copy(land, land, v_sems.at[i], s, s, s).wait_recv()
        vist[:, columns_of(s)] = visl[s].T.astype(BF16)

    vist[:, columns_of(me)] = visf[me].T.astype(BF16)
    far = range(nh - 1, 0, -1)
    left = list(range(1, n))
    done = set()
    for step, d in enumerate(far):
        for way, at in ((0, d), (1, nh - 1 - d)):
            if at not in done:
                visual_term(at)
                done.add(at)
        for i in range(PIECES):
            for way, at in ((0, d), (1, nh - 1 - d)):
                relay(way, at, i)
    for k in left:
        take_visual(k)

    forward(agl, ag_sems, on_sems.at[1])
    wait_rest(agl, ag_sems)
    for i, out in enumerate((kwg_out, vwg_out)):
        out[...] = jnp.dot(
            vist[...], agl[:, i].reshape(n * rows, cols).astype(BF16), preferred_element_type=F32
        )
    wait_all(qgl, qg_sems)
    for s in range(n):
        part, block = s % split, s // split
        qg_out[
            part * text_part : (part + 1) * text_part, block * width : (block + 1) * width
        ] = qgl[s]

    vg_out[...] = vgp[my_head]
    for way, land in ((0, zr), (1, zl)):

        @pl.when(takes_from(way))
        def _():
            for i in range(PIECES):
                hop(way, my_head, i).wait_recv()
            vg_out[...] += land[my_head]

        for d in range(nh):

            @pl.when(sends_to(way, d))
            def _():
                for i in range(PIECES):
                    hop(way, d, i).wait_send()

    for copy in sends:
        copy.wait_send()


def solution(mesh):
    n, nh = mesh.shape["frame"], mesh.shape["head"]

    def body(visual, w_key, w_value, queries, out_grad):
        rows, depth = visual.shape
        cols = w_key.shape[1]
        text, query_cols = queries.shape
        local_heads = query_cols // HEAD_DIM
        split = max(1, n // local_heads)
        part, width = text // split, query_cols * split // n
        vmem = pl.BlockSpec(memory_space=pltpu.VMEM)
        hbm = pl.BlockSpec(memory_space=pl.ANY)
        dn, dh = depth // n, depth // nh
        pairs = pltpu.SemaphoreType.DMA((2, n))
        return pl.pallas_call(
            functools.partial(kernel, n, nh),
            out_shape=(
                jax.ShapeDtypeStruct((text, query_cols), F32),
                jax.ShapeDtypeStruct((dn, cols), F32),
                jax.ShapeDtypeStruct((dn, cols), F32),
                jax.ShapeDtypeStruct((rows, dh), F32),
            ),
            in_specs=[vmem, hbm, hbm, vmem, vmem],
            out_specs=(vmem, vmem, vmem, vmem),
            scratch_shapes=[
                pltpu.VMEM((depth, cols), BF16),
                pltpu.VMEM((depth, cols), BF16),
                pltpu.VMEM((n, rows, dn), F32),
                pltpu.VMEM((n, rows, dn), F32),
                pltpu.VMEM((dn, n * rows), BF16),
                pltpu.VMEM((n, part, width), F32),
                pltpu.VMEM((n, part, width), F32),
                pltpu.VMEM((cols // HEAD_DIM, 2, rows, HEAD_DIM), F32),
                pltpu.VMEM((n, 2, rows, HEAD_DIM), F32),
                pltpu.VMEM((2, n // 2, 2, rows, HEAD_DIM), F32),
                pltpu.VMEM((n // 2, 2, rows, HEAD_DIM), F32),
                pltpu.VMEM((n // 2, 2, rows, HEAD_DIM), F32),
                pltpu.VMEM((2, rows, cols), F32),
                pltpu.VMEM((n, 2, rows, cols), F32),
                pltpu.VMEM((n, part, width), F32),
                pltpu.VMEM((n, part, width), F32),
                pltpu.VMEM((nh, rows, dh), F32),
                pltpu.VMEM((nh, rows, dh), F32),
                pltpu.VMEM((nh, rows, dh), F32),
                pltpu.SemaphoreType.DMA((2, CHUNKS)),
                pairs, pairs, pairs,
                pltpu.SemaphoreType.DMA((3, 2, n)),
                pltpu.SemaphoreType.DMA((2,)),
                pltpu.SemaphoreType.DMA((2, n // 2)),
                pairs, pairs, pairs,
                pltpu.SemaphoreType.DMA((2, 2, nh, PIECES)),
            ],
            compiler_params=pltpu.CompilerParams(
                collective_id=0, has_side_effects=True, vmem_limit_bytes=67000000
            ),
        )(visual, w_key, w_value, queries, out_grad)

    return jax.shard_map(
        body,
        mesh=mesh,
        in_specs=(
            P("frame", None),
            P(None, "head"),
            P(None, "head"),
            P("frame", "head"),
            P("frame", "head"),
        ),
        out_specs=(P("frame", "head"), P("frame", "head"), P("frame", "head"), P("frame", "head")),
        check_vma=False,
    )
```

```python
import functools

import jax
import jax.numpy as jnp
from jax import lax
from jax.experimental import pallas as pl
from jax.experimental.pallas import tpu as pltpu
from jax.sharding import PartitionSpec as P

HEAD_DIM = 128
MESH = pl.DeviceIdType.MESH
CHUNKS = 8
PIECES = 4
F32, BF16 = jnp.float32, jnp.bfloat16


def halves(a):
    high = a.astype(BF16)
    return high, (a - high.astype(F32)).astype(BF16)


def product(a, b, dims):
    (ah, al), (bh, bl) = a, b
    dot = functools.partial(
        lax.dot_general, dimension_numbers=(dims, ((), ())), preferred_element_type=F32
    )
    return dot(ah, bh) + (dot(ah, bl) + dot(al, bh))


def kernel(
    n, nh, vis, wk_any, wv_any, q, g, qg_out, kwg_out, vwg_out, vg_out,
    wk, wv, visf, visl, vist, ql, gl, kvs, kvl, parts, pre, partl, kgs, agl, qgs, qgl, vgp, zr, zl,
    w_sem, q_sems, g_sems, kv_sems, v_sems, pre_sem, part_sems, qg_sems, ag_sems, on_sems, z_sems,
):
    me, my_head = lax.axis_index("frame"), lax.axis_index("head")
    rows, depth = vis.shape
    cols = wk.shape[1]
    kv_local = cols // HEAD_DIM
    text_part, width = ql.shape[1], ql.shape[2]
    split = q.shape[0] // text_part
    heads = width // HEAD_DIM
    share = n // kv_local
    dn, dh = depth // n, depth // nh
    chunk = depth // CHUNKS
    bounds = (0, rows)
    piece = rows // PIECES
    factor = HEAD_DIM ** (-0.5)

    def frame_copy(src, dst, sems, slot_send, slot_recv, target):
        return pltpu.make_async_remote_copy(
            src_ref=src, dst_ref=dst, send_sem=sems.at[0, slot_send],
            recv_sem=sems.at[1, slot_recv], device_id={"frame": target}, device_id_type=MESH,
        )

    def frame_copy_of(src, dst, send_sem, recv_sem, target):
        return pltpu.make_async_remote_copy(
            src_ref=src, dst_ref=dst, send_sem=send_sem, recv_sem=recv_sem,
            device_id={"frame": target}, device_id_type=MESH,
        )

    def peer(k):
        return lax.rem(me + k, n)

    def source(k):
        return lax.rem(me + n - k, n)

    core, chip, chips = lax.rem(me, 2), me // 2, n // 2
    sibling = me + 1 - 2 * core

    def mate(j):
        return lax.rem(me + 2 * j, n)

    def mate_source(j):
        return lax.rem(me + n - 2 * j, n)

    def onward(land, sems, on, s):
        return frame_copy_of(land.at[s], land.at[s], on.at[s], sems.at[1, s], sibling)

    def spread(pick, land, sems):
        sends.append(frame_copy(pick(sibling), land.at[me], sems, sibling, me, sibling))
        sends[-1].start()
        for j in range(1, chips):
            p = mate(j)
            sends.append(frame_copy(pick(p), land.at[me], sems, p, me, p))
            sends[-1].start()

    def forward(land, sems, on):
        for j in range(1, chips):
            s = mate_source(j)
            frame_copy(land.at[s], land.at[s], sems, s, s, s).wait_recv()
            sends.append(onward(land, sems, on, s))
            sends[-1].start()

    def wait_rest(land, sems):
        frame_copy(land.at[sibling], land.at[sibling], sems, sibling, sibling, sibling).wait_recv()
        for j in range(1, chips):
            s = lax.rem(sibling + n - 2 * j, n)
            frame_copy(land.at[s], land.at[s], sems, s, s, sibling).wait_recv()

    loads = []
    for c in range(CHUNKS):
        at = pl.ds(c * chunk, chunk)
        for i, (src, dst) in enumerate(((wk_any, wk), (wv_any, wv))):
            loads.append(pltpu.make_async_copy(src.at[at], dst.at[at], w_sem.at[i, c]))
            loads[-1].start()

    barrier = pltpu.get_barrier_semaphore()
    for k in range(1, n):
        pl.semaphore_signal(barrier, inc=1, device_id={"frame": peer(k)}, device_id_type=MESH)
    for j in range(1, nh):
        pl.semaphore_signal(
            barrier, inc=1, device_id={"head": lax.rem(my_head + j, nh)}, device_id_type=MESH
        )
    pl.semaphore_wait(barrier, n + nh - 2)

    def text_at(p):
        part, block = lax.rem(p, split), p // split
        return (
            pl.ds(pl.multiple_of(part * text_part, text_part), text_part),
            pl.ds(pl.multiple_of(block * width, width), width),
        )

    sends = []
    for k in range(1, n):
        p = peer(k)
        for src, dst, sems in ((q, ql, q_sems), (g, gl, g_sems)):
            sends.append(frame_copy(src.at[text_at(p)], dst.at[me], sems, p, me, p))
            sends[-1].start()
    ql[me] = q[text_at(me)]
    gl[me] = g[text_at(me)]

    def stretch(i):
        return pl.ds(bounds[i], bounds[i + 1] - bounds[i])

    def send_visual(i):
        for k in range(1, n):
            p = peer(k)
            sends.append(
                frame_copy(
                    visf.at[p, stretch(i)], visl.at[me, stretch(i)], v_sems.at[i], p, me, p
                )
            )
            sends[-1].start()

    acc_k = acc_v = jnp.zeros((rows, cols), F32)
    for c in range(CHUNKS):
        loads[2 * c].wait()
        loads[2 * c + 1].wait()
        at = pl.ds(c * chunk, chunk)
        acc_k += jnp.dot(vis[:, at], wk[at], preferred_element_type=F32)
        acc_v += jnp.dot(vis[:, at], wv[at], preferred_element_type=F32)
    for a in range(kv_local):
        at = slice(a * HEAD_DIM, (a + 1) * HEAD_DIM)
        kvs[a, 0] = acc_k[:, at]
        kvs[a, 1] = acc_v[:, at]
    spread(lambda p: kvs.at[p // share], kvl, kv_sems)
    kvl[me] = kvs[me // share]


    def wait_all(land, sems):
        for k in range(1, n):
            s = source(k)
            frame_copy(land.at[s], land.at[s], sems, s, s, s).wait_recv()

    for p in range(n):
        visf[p] = vis[:, p * dn : (p + 1) * dn].astype(F32)
    forward(kvl, kv_sems, on_sems.at[0])
    wait_all(ql, q_sems)
    wait_all(gl, g_sems)
    wait_rest(kvl, kv_sems)

    keys = kvl[:, 0].reshape(n * rows, HEAD_DIM)
    values = kvl[:, 1].reshape(n * rows, HEAD_DIM)
    values2 = halves(values)
    keys_t = halves(keys.T)
    key_part = value_part = None
    for h in range(heads):
        at = slice(h * HEAD_DIM, (h + 1) * HEAD_DIM)
        query = ql[:, :, at].reshape(n * text_part, HEAD_DIM)
        grad = gl[:, :, at].reshape(n * text_part, HEAD_DIM)
        query2, grad2 = halves(query), halves(grad)
        scores = lax.dot_general(
            keys, query, (((1,), (1,)), ((), ())),
            precision=lax.Precision.HIGHEST, preferred_element_type=F32,
        ) * factor
        probs = jnp.exp(scores - jnp.max(scores, axis=0, keepdims=True))
        probs = probs * (1.0 / jnp.sum(probs, axis=0, keepdims=True))
        dprob = product(values2, grad2, ((1,), (1,)))
        delta = jnp.sum(probs * dprob, axis=0, keepdims=True)
        dscore2 = halves(probs * (dprob - delta))
        key_term = product(dscore2, query2, ((1,), (0,)))
        value_term = product(halves(probs), grad2, ((1,), (0,)))
        key_part = key_term if h == 0 else key_part + key_term
        value_part = value_term if h == 0 else value_part + value_term
        query_term = product(keys_t, dscore2, ((1,), (0,))).T * factor
        qgs[:, :, at] = query_term.reshape(n, text_part, HEAD_DIM)
    for i, part in enumerate((key_part, value_part)):
        part = part.reshape(chips, 2, rows, HEAD_DIM)
        for c in range(2):
            parts[c, :, i] = part[:, c]
    exchange = frame_copy_of(
        parts.at[1 - core], pre, pre_sem.at[0], pre_sem.at[1], sibling
    )
    exchange.start()
    exchange.wait_recv()
    sends.append(exchange)
    parts[core] += pre[...]
    for j in range(1, chips):
        p = mate(j)
        sends.append(
            frame_copy(parts.at[core, p // 2], partl.at[chip], part_sems, p // 2, chip, p)
        )
        sends[-1].start()
    partl[chip] = parts[core, chip]
    for k in range(1, n):
        p = peer(k)
        sends.append(frame_copy(qgs.at[p], qgl.at[me], qg_sems, p, me, p))
        sends[-1].start()
    qgl[me] = qgs[me]
    send_visual(0)

    for j in range(1, chips):
        s = mate_source(j)
        land = partl.at[s // 2]
        frame_copy(land, land, part_sems, s // 2, s // 2, s).wait_recv()
    low = []
    for i in range(2):
        columns = []
        for a in range(kv_local):
            total = partl[a * share // 2, i]
            for p in range(a * share // 2 + 1, (a + 1) * share // 2):
                total = total + partl[p, i]
            columns.append(total * factor if i == 0 else total)
        for a in range(kv_local):
            kgs[i, :, a * HEAD_DIM : (a + 1) * HEAD_DIM] = columns[a].astype(BF16).astype(F32)
        low.append(kgs[i].astype(BF16))

    spread(lambda p: kgs, agl, ag_sems)
    agl[me] = kgs[...]

    def visual_term(p):
        at = slice(p * dh, (p + 1) * dh)
        dims = (((1,), (1,)), ((), ()))
        vgp[p] = lax.dot_general(
            low[0], wk[at], dims, preferred_element_type=F32
        ) + lax.dot_general(low[1], wv[at], dims, preferred_element_type=F32)

    def hop(way, d, i):
        at = pl.ds(i * piece, piece)
        land = zr if way == 0 else zl
        return pltpu.make_async_remote_copy(
            src_ref=vgp.at[d, at], dst_ref=land.at[d, at], send_sem=z_sems.at[way, 0, d, i],
            recv_sem=z_sems.at[way, 1, d, i], device_id_type=MESH,
            device_id={"head": jnp.clip(my_head + 1 - 2 * way, 0, nh - 1)},
        )

    def sends_to(way, d):
        return my_head < d if way == 0 else my_head > d

    def takes_from(way):
        return my_head > 0 if way == 0 else my_head < nh - 1

    def relay(way, d, i):
        at = pl.ds(i * piece, piece)
        land = zr if way == 0 else zl

        @pl.when(sends_to(way, d))
        def _():
            @pl.when(takes_from(way))
            def _():
                hop(way, d, i).wait_recv()
                vgp[d, at] += land[d, at]

            hop(way, d, i).start()

    def columns_of(s):
        return pl.ds(pl.multiple_of(s * rows, rows), rows)

    def take_visual(k):
        s = source(k)
        for i in range(1):
            land = visl.at[s, stretch(i)]
            frame_copy(land, land, v_sems.at[i], s, s, s).wait_recv()
        vist[:, columns_of(s)] = visl[s].T.astype(BF16)

    vist[:, columns_of(me)] = visf[me].T.astype(BF16)
    far = range(nh - 1, 0, -1)
    left = list(range(1, n))
    done = set()
    for step, d in enumerate(far):
        for way, at in ((0, d), (1, nh - 1 - d)):
            if at not in done:
                visual_term(at)
                done.add(at)
        for i in range(PIECES):
            for way, at in ((0, d), (1, nh - 1 - d)):
                relay(way, at, i)
    for k in left:
        take_visual(k)

    forward(agl, ag_sems, on_sems.at[1])
    wait_rest(agl, ag_sems)
    for i, out in enumerate((kwg_out, vwg_out)):
        out[...] = jnp.dot(
            vist[...], agl[:, i].reshape(n * rows, cols).astype(BF16), preferred_element_type=F32
        )
    wait_all(qgl, qg_sems)
    for s in range(n):
        part, block = s % split, s // split
        qg_out[
            part * text_part : (part + 1) * text_part, block * width : (block + 1) * width
        ] = qgl[s]

    vg_out[...] = vgp[my_head]
    for way, land in ((0, zr), (1, zl)):

        @pl.when(takes_from(way))
        def _():
            for i in range(PIECES):
                hop(way, my_head, i).wait_recv()
            vg_out[...] += land[my_head]

        for d in range(nh):

            @pl.when(sends_to(way, d))
            def _():
                for i in range(PIECES):
                    hop(way, d, i).wait_send()

    for copy in sends:
        copy.wait_send()


def solution(mesh):
    n, nh = mesh.shape["frame"], mesh.shape["head"]

    def body(visual, w_key, w_value, queries, out_grad):
        rows, depth = visual.shape
        cols = w_key.shape[1]
        text, query_cols = queries.shape
        local_heads = query_cols // HEAD_DIM
        split = max(1, n // local_heads)
        part, width = text // split, query_cols * split // n
        vmem = pl.BlockSpec(memory_space=pltpu.VMEM)
        hbm = pl.BlockSpec(memory_space=pl.ANY)
        dn, dh = depth // n, depth // nh
        pairs = pltpu.SemaphoreType.DMA((2, n))
        return pl.pallas_call(
            functools.partial(kernel, n, nh),
            out_shape=(
                jax.ShapeDtypeStruct((text, query_cols), F32),
                jax.ShapeDtypeStruct((dn, cols), F32),
                jax.ShapeDtypeStruct((dn, cols), F32),
                jax.ShapeDtypeStruct((rows, dh), F32),
            ),
            in_specs=[vmem, hbm, hbm, vmem, vmem],
            out_specs=(vmem, vmem, vmem, vmem),
            scratch_shapes=[
                pltpu.VMEM((depth, cols), BF16),
                pltpu.VMEM((depth, cols), BF16),
                pltpu.VMEM((n, rows, dn), F32),
                pltpu.VMEM((n, rows, dn), F32),
                pltpu.VMEM((dn, n * rows), BF16),
                pltpu.VMEM((n, part, width), F32),
                pltpu.VMEM((n, part, width), F32),
                pltpu.VMEM((cols // HEAD_DIM, 2, rows, HEAD_DIM), F32),
                pltpu.VMEM((n, 2, rows, HEAD_DIM), F32),
                pltpu.VMEM((2, n // 2, 2, rows, HEAD_DIM), F32),
                pltpu.VMEM((n // 2, 2, rows, HEAD_DIM), F32),
                pltpu.VMEM((n // 2, 2, rows, HEAD_DIM), F32),
                pltpu.VMEM((2, rows, cols), F32),
                pltpu.VMEM((n, 2, rows, cols), F32),
                pltpu.VMEM((n, part, width), F32),
                pltpu.VMEM((n, part, width), F32),
                pltpu.VMEM((nh, rows, dh), F32),
                pltpu.VMEM((nh, rows, dh), F32),
                pltpu.VMEM((nh, rows, dh), F32),
                pltpu.SemaphoreType.DMA((2, CHUNKS)),
                pairs, pairs, pairs,
                pltpu.SemaphoreType.DMA((1, 2, n)),
                pltpu.SemaphoreType.DMA((2,)),
                pltpu.SemaphoreType.DMA((2, n // 2)),
                pairs, pairs, pairs,
                pltpu.SemaphoreType.DMA((2, 2, nh, PIECES)),
            ],
            compiler_params=pltpu.CompilerParams(
                collective_id=0, has_side_effects=True, vmem_limit_bytes=67000000
            ),
        )(visual, w_key, w_value, queries, out_grad)

    return jax.shard_map(
        body,
        mesh=mesh,
        in_specs=(
            P("frame", None),
            P(None, "head"),
            P(None, "head"),
            P("frame", "head"),
            P("frame", "head"),
        ),
        out_specs=(P("frame", "head"), P("frame", "head"), P("frame", "head"), P("frame", "head")),
        check_vma=False,
    )
```
